32 devices in a mesh: groups: 2 (over x), tm: 8 (over z, y), tile: 2 (over core).
Axes of the slice: x: 2, y: 2, z: 4, core: 2. Of those that a mesh axis runs over, the one named last changes fastest.
Arguments:
- frames: bfloat16 [2, 16, 2, 64, 2048], P(None, ('groups', 'tm'), 'tile'), parts along dimension 1, may hold values from -6 to 6
- forward_carry: bfloat16 [16, 2, 64, 2048], P(('groups', 'tm'), 'tile'), parts along dimension 0, may hold values from -6 to 6
- backward_carry: bfloat16 [16, 2, 64, 2048], P(('groups', 'tm'), 'tile'), parts along dimension 0, may hold values from -6 to 6
- forward_source: int32 [2, 16, 32], P(None, ('groups', 'tm'), 'tile'), parts along dimension 1, may hold values from 0 to 31, as said below
- backward_source: int32 [2, 16, 32], P(None, ('groups', 'tm'), 'tile'), parts along dimension 1, may hold values from 0 to 31, as said below
- forward_entry: bfloat16 [9, 64, 128], replicated, may hold values from -0.1875 to 0.1875
- forward_blocks: bfloat16 [1, 2, 9, 64, 64], replicated, may hold values from -0.25 to 0.25
- backward_entry: bfloat16 [9, 64, 128], replicated, may hold values from -0.1875 to 0.1875
- backward_blocks: bfloat16 [1, 2, 9, 64, 64], replicated, may hold values from -0.25 to 0.25
- mixing_weight: bfloat16 [64, 128], replicated, may hold values from -0.5 to 0.5
Outputs:
- restored: bfloat16 [2, 16, 2, 64, 2048], P(None, ('groups', 'tm'), 'tile'), parts along dimension 1
- forward_final: bfloat16 [16, 2, 64, 2048], P(('groups', 'tm'), 'tile'), parts along dimension 0
- backward_final: bfloat16 [16, 2, 64, 2048], P(('groups', 'tm'), 'tile'), parts along dimension 0
The draws below stay inside these ranges and needn't reach their ends.
There are 2 independent parts, one for each index of `groups`. The reference program is written for one: setup_inputs(seed, part) draws one part's arguments, and reference() takes and returns one part's arrays. A program takes and returns all parts, laid end to end along the dimension named above; an argument that names none is the same for every part. Nothing has to cross between parts.
Inputs may be any that keep to these rules, and one draw needn't show every extreme that they name: `forward_source`: for each step, segment and destination block of a frame, the block whose forward features it takes: the destination moved by at most one block row and three block columns, kept inside the frame. `backward_source`: the same for backward features.
All inputs are finite; a program needn't handle non-finite values.
Results may differ from the reference program's by a relative error of at most 0.012.
Values may be sent and summed in bfloat16 or wider, within the bound.
A program may use at most 64 MiB of HBM per device.

```python
import jax
import jax.numpy as jnp
from jax import lax

C = 64
RH = 32
RW = 64
BH = 8
BW = 16
NB = 1
TICKS = 2
SEGMENTS = 8
NREG = 2
BLOCKS = 32


def source_draw(key):
    block_rows = RH // BH
    block_cols = RW // BW
    per_region = block_rows * block_cols
    positions = jnp.arange(BLOCKS, dtype=jnp.int32)
    region = positions // per_region
    within = positions % per_region
    dest_row = within // block_cols
    dest_col = region * block_cols + within % block_cols
    row_key, col_key = jax.random.split(key)
    draw_shape = (TICKS, SEGMENTS, BLOCKS)
    row_move = jax.random.randint(row_key, draw_shape, -1, 2).astype(jnp.int32)
    col_move = jax.random.randint(col_key, draw_shape, -3, 4).astype(jnp.int32)
    final_block = positions == BLOCKS - 1
    start_block = positions == 0
    row_move = jnp.where(final_block, jnp.abs(row_move), jnp.where(start_block, -jnp.abs(row_move), row_move))
    col_move = jnp.where(final_block, jnp.abs(col_move), jnp.where(start_block, -jnp.abs(col_move), col_move))
    src_row = jnp.clip(dest_row + row_move, 0, block_rows - 1)
    src_col = jnp.clip(dest_col + col_move, 0, NREG * block_cols - 1)
    return (src_col // block_cols * per_region + src_row * block_cols + src_col % block_cols).astype(jnp.int32)


def draw_forward_source(key, part):
    return source_draw(jax.random.fold_in(key, 11))


def draw_backward_source(key, part):
    return source_draw(jax.random.fold_in(key, 23))


def level_of(rng, extent, shards, smallest, largest):
    gain = 1.0
    for dim, shards_of in shards:
        steps = jax.random.uniform(jax.random.fold_in(jax.random.fold_in(rng, 6), dim), (shards_of,), jnp.float32, smallest / len(shards), largest / len(shards))
        gain = gain * jnp.repeat(jnp.exp(steps), extent[dim] // shards_of).reshape((-1,) + (1,) * (len(extent) - 1 - dim))
    return gain


def noise(stream_key, dims, width, reach, cuts=(), kind=jnp.bfloat16):
    drawn = jax.random.normal(stream_key, dims, jnp.float32) * width
    if len(cuts) > 0:
        drawn = level_of(stream_key, dims, cuts, -0.22, 0.18) * drawn
    return jnp.clip(drawn, min=-reach, max=reach).astype(kind)


def setup_inputs(seed: int = 0, part: int = 0) -> dict:
    key_list = jax.random.split(jax.random.key(seed), 11)
    part_keys = jax.random.split(jax.random.fold_in(key_list[10], part), 11)
    return {
        "frames": noise(part_keys[0], (TICKS, SEGMENTS, NREG, C, RH * RW), 1.0, 6.0, ((1, 8), (2, 2))),
        "forward_carry": noise(part_keys[1], (SEGMENTS, NREG, C, RH * RW), 1.0, 6.0, ((0, 8), (1, 2))),
        "backward_carry": noise(part_keys[2], (SEGMENTS, NREG, C, RH * RW), 1.0, 6.0, ((0, 8), (1, 2))),
        "forward_source": draw_forward_source(jax.random.fold_in(jax.random.fold_in(key_list[10], part), 71), part),
        "backward_source": draw_backward_source(jax.random.fold_in(jax.random.fold_in(key_list[10], part), 71), part),
        "forward_entry": noise(key_list[5], (9, C, 2 * C), (18 * C) ** -0.5, 0.1875),
        "forward_blocks": noise(key_list[6], (NB, 2, 9, C, C), (9 * C) ** -0.5, 0.25),
        "backward_entry": noise(key_list[7], (9, C, 2 * C), (18 * C) ** -0.5, 0.1875),
        "backward_blocks": noise(key_list[8], (NB, 2, 9, C, C), (9 * C) ** -0.5, 0.25),
        "mixing_weight": noise(key_list[9], (C, 2 * C), (2 * C) ** -0.5, 0.5),
    }


def convolve(feature, weight):
    regions, channels, pixels = feature.shape
    grid = feature.astype(jnp.float32).reshape(regions, channels, RH, RW)
    padded = jnp.pad(grid, ((0, 0), (0, 0), (1, 1), (1, 1)))
    summed = jnp.zeros((regions, weight.shape[1], pixels), jnp.float32)
    for kernel_tap in range(9):
        row_off = kernel_tap // 3
        col_off = kernel_tap % 3
        window = padded[:, :, row_off:row_off + RH, col_off:col_off + RW].reshape(regions, channels, pixels)
        summed = summed + jnp.einsum("oi,rip->rop", weight[kernel_tap].astype(jnp.float32), window, precision=lax.Precision.HIGHEST)
    return summed


def to_blocks(feature):
    regions, channels, pixels = feature.shape
    grid = feature.reshape(regions, channels, RH // BH, BH, RW // BW, BW)
    grid = grid.transpose(0, 2, 4, 1, 3, 5)
    return grid.reshape(regions * (RH // BH) * (RW // BW), channels, BH * BW)


def from_blocks(blocks, regions):
    channels = blocks.shape[1]
    grid = blocks.reshape(regions, RH // BH, RW // BW, channels, BH, BW)
    grid = grid.transpose(0, 3, 1, 4, 2, 5)
    return grid.reshape(regions, channels, RH * RW)


def warp_blocks(whole_frame, sources):
    per_region = (RH // BH) * (RW // BW)
    picked = jnp.take(to_blocks(whole_frame), sources, axis=0)
    return from_blocks(picked, sources.shape[0] // per_region)


def propagate(frame_now, warped, entry, layers):
    joined = jnp.concatenate([frame_now, warped], axis=1)
    hidden = jax.nn.leaky_relu(convolve(joined, entry), 0.1).astype(jnp.bfloat16)
    for layer in range(layers.shape[0]):
        inner = jax.nn.leaky_relu(convolve(hidden, layers[layer, 0]), 0.1).astype(jnp.bfloat16)
        hidden = (hidden.astype(jnp.float32) + convolve(inner, layers[layer, 1])).astype(jnp.bfloat16)
    return hidden


def reference(frames, forward_carry, backward_carry, forward_source, backward_source, forward_entry, forward_blocks, backward_entry, backward_blocks, mixing_weight):
    forward_state = forward_carry
    backward_state = backward_carry
    segments, regions, channels, pixels = forward_carry.shape
    results = []
    for moment in range(TICKS):
        frame_now = frames[moment].reshape(segments * regions, channels, pixels)
        empty = jnp.zeros_like(forward_state[:1])
        came_forward = jnp.concatenate([empty, forward_state[:-1]], axis=0)
        came_backward = jnp.concatenate([backward_state[1:], empty], axis=0)
        warped_forward = jax.vmap(warp_blocks)(came_forward, forward_source[moment])
        warped_backward = jax.vmap(warp_blocks)(came_backward, backward_source[moment])
        new_forward = propagate(frame_now, warped_forward.reshape(segments * regions, channels, pixels), forward_entry, forward_blocks)
        new_backward = propagate(frame_now, warped_backward.reshape(segments * regions, channels, pixels), backward_entry, backward_blocks)
        both = jnp.concatenate([new_forward, new_backward], axis=1).astype(jnp.float32)
        mixed = jnp.einsum("oi,rip->rop", mixing_weight.astype(jnp.float32), both, precision=lax.Precision.HIGHEST)
        results.append((frame_now.astype(jnp.float32) + mixed).astype(jnp.bfloat16).reshape(segments, regions, channels, pixels))
        forward_state = new_forward.reshape(segments, regions, channels, pixels)
        backward_state = new_backward.reshape(segments, regions, channels, pixels)
    return jnp.stack(results), forward_state, backward_state
```

```python
import functools

import jax
import jax.numpy as jnp
from jax import lax
from jax.experimental import pallas as pl
from jax.experimental.pallas import tpu as pltpu
from jax.sharding import PartitionSpec as P

RH = 32
RW = 64
BH = 8
BW = 16
LANES = 128
TILES = RH * RW // LANES
GROUP = 4
PACK = 16
CHUNKS = 2
MESH = pl.DeviceIdType.MESH
F32 = jnp.float32
BF16 = jnp.bfloat16


def lrelu(value):
    return jnp.maximum(value, 0.1 * value)


def stacked(piece):
    return jnp.concatenate(
        [jnp.concatenate([piece(3 * a + b) for a in range(3)], axis=1) for b in range(3)], axis=0
    )


def lane_of(rows):
    return lax.broadcasted_iota(jnp.int32, (rows, LANES), 1)


def convolve(source, weight, finish):
    channels = source.shape[0]
    lane = lane_of(channels)
    first_half = lane < RW
    column = lane % RW
    outs = weight.shape[0] // (3 * channels)

    def step(group, _):
        start = pl.multiple_of(group * (GROUP * LANES), GROUP * LANES)
        window = source[:, pl.ds(start, (GROUP + 2) * LANES)]
        tiles = [window[:, t * LANES:(t + 1) * LANES] for t in range(GROUP + 2)]
        turned = [pltpu.roll(tile, RW, 1) for tile in tiles]
        between = [jnp.where(first_half, turned[t], turned[t + 1]) for t in range(GROUP + 1)]
        rhs = jnp.concatenate(
            [
                jnp.concatenate(between[:-1], axis=1),
                jnp.concatenate(tiles[1:-1], axis=1),
                jnp.concatenate(between[1:], axis=1),
            ],
            axis=0,
        )
        product = jnp.dot(weight[...], rhs, preferred_element_type=F32)
        for t in range(GROUP):
            sums = []
            for o in range(outs):
                left, mid, right = (
                    product[(3 * o + b) * channels:(3 * o + b + 1) * channels, t * LANES:(t + 1) * LANES]
                    for b in range(3)
                )
                left = jnp.where(column == 0, 0.0, pltpu.roll(left, 1, 1))
                right = jnp.where(column == RW - 1, 0.0, pltpu.roll(right, LANES - 1, 1))
                sums.append(mid + left + right)
            finish(group * GROUP + t, sums)
        return _

    lax.fori_loop(0, TILES // GROUP, step, 0)


def at_tile(tile, padded):
    return pl.ds(pl.multiple_of((tile + padded) * LANES, LANES), LANES)


def turned_columns(tile, steps, lane):
    if steps == 0:
        return tile
    shift = steps * BW
    inside = pltpu.roll(tile, shift, 1)
    wrapped = pltpu.roll(tile, (shift - RW) % LANES, 1)
    return jnp.where(lane % RW >= shift, inside, wrapped)


def by_column(block_of_lane, values):
    spread = jnp.full(block_of_lane.shape, values[0], jnp.int32)
    for q in range(1, len(values)):
        spread = jnp.where(block_of_lane == q, values[q], spread)
    return spread


def warp(arrived, sources, moment, target):
    channels = target.shape[0]
    cols = RW // BW
    rows = RH // BH
    tiles_of_block = BH * RW // LANES
    lane = lane_of(PACK)
    block_of_lane = lane % RW // BW

    def step(row, _):
        regions, moves, turns = [], [], []
        for col in range(cols):
            block = sources[moment, row * cols + col]
            within = lax.rem(block, rows * cols)
            regions.append(lax.div(block, rows * cols))
            moves.append(lax.div(within, cols) - row)
            turns.append(lax.rem(col - lax.rem(within, cols) + cols, cols))
        turn = by_column(block_of_lane, turns)
        picks = []
        for steps in range(cols):
            order = [(q + steps) % cols for q in range(cols)]
            region = by_column(block_of_lane, [regions[c] for c in order])
            move = by_column(block_of_lane, [moves[c] for c in order])
            picks.append((region == 1, move < 0, move > 0, turn == steps))
        near = (jnp.maximum(row - 1, 0), row, jnp.minimum(row + 1, rows - 1))
        for t in range(tiles_of_block):
            for part in range(channels // PACK):
                held = pl.ds(part * PACK, PACK)
                tiles = [
                    [arrived[region, held, at_tile(near_row * tiles_of_block + t, 0)] for region in range(2)]
                    for near_row in near
                ]
                result = None
                for steps in range(cols):
                    second, above, below, wanted = picks[steps]
                    up, same, down = (jnp.where(second, pair[1], pair[0]) for pair in tiles)
                    moved = jnp.where(above, up, jnp.where(below, down, same))
                    moved = turned_columns(moved, steps, lane)
                    result = moved if result is None else jnp.where(wanted, moved, result)
                target[held, at_tile(row * tiles_of_block + t, 1)] = result
        return _

    lax.fori_loop(0, rows, step, 0)


def kernel(
    count,
    frames,
    carry_f,
    carry_b,
    src_f,
    src_b,
    entry_f,
    blocks_f,
    entry_b,
    blocks_b,
    mixing,
    restored,
    final_f,
    final_b,
    arrived_0f,
    arrived_0b,
    arrived_1f,
    arrived_1b,
    state,
    padded,
    hidden,
    inner,
    pre,
    frame_w,
    warp_w,
    block_w,
    send_sem,
    recv_sem,
    pass_sem,
    got_sem,
):
    ticks, channels, pixels = frames.shape
    arrived = ((arrived_0f, arrived_0b), (arrived_1f, arrived_1b))
    me = lax.axis_index("tm")
    side = lax.axis_index("tile")
    other = 1 - side
    to = (me + 1, me - 1)
    has_to = (me < count - 1, me > 0)
    has_from = (me > 0, me < count - 1)

    barrier = pltpu.get_barrier_semaphore()
    pl.semaphore_signal(barrier, inc=1, device_id={"tile": other}, device_id_type=MESH)
    for d in range(2):
        @pl.when(has_to[d])
        def _(d=d):
            pl.semaphore_signal(barrier, inc=1, device_id={"tm": to[d]}, device_id_type=MESH)
    pl.semaphore_wait(barrier, 1 + jnp.minimum(me, 1) + jnp.minimum(count - 1 - me, 1))

    part = channels // CHUNKS

    def sending(moment, d, chunk):
        rows = pl.ds(chunk * part, part)
        origin = (carry_f, carry_b)[d].at[rows] if moment == 0 else state.at[d, rows]
        return pltpu.make_async_remote_copy(
            src_ref=origin,
            dst_ref=arrived[moment][d].at[side, rows],
            send_sem=send_sem.at[moment, d, chunk],
            recv_sem=recv_sem.at[moment, d, chunk],
            device_id={"tm": to[d]},
            device_id_type=MESH,
        )

    def passing(moment, d, chunk):
        rows = pl.ds(chunk * part, part)
        return pltpu.make_async_remote_copy(
            src_ref=arrived[moment][d].at[side, rows],
            dst_ref=arrived[moment][d].at[side, rows],
            send_sem=pass_sem.at[moment, d, chunk],
            recv_sem=got_sem.at[moment, d, chunk],
            device_id={"tile": other},
            device_id_type=MESH,
        )

    def send(moment, d):
        @pl.when(has_to[d])
        def _():
            for chunk in range(CHUNKS):
                sending(moment, d, chunk).start()

    def receive(moment, d):
        @pl.when(has_from[d])
        def _():
            for chunk in range(CHUNKS):
                sending(moment, d, chunk).wait_recv()
                passing(moment, d, chunk).start()
            for chunk in range(CHUNKS):
                passing(moment, d, chunk).wait_recv()

    send(0, 0)
    send(0, 1)

    for d in range(2):
        @pl.when(jnp.logical_not(has_from[d]))
        def _(d=d):
            for moment in range(ticks):
                for region in range(2):
                    arrived[moment][d][region] = jnp.zeros((channels, pixels), BF16)
    edge = jnp.zeros((channels, LANES), BF16)
    for buffer in (padded, hidden, inner):
        buffer[:, :LANES] = edge
        buffer[:, (TILES + 1) * LANES:] = edge
    for d, (entry, blocks) in enumerate(((entry_f, blocks_f), (entry_b, blocks_b))):
        frame_w[3 * channels * d:3 * channels * (d + 1)] = stacked(lambda tap: entry[tap, :, :channels])
        warp_w[d] = stacked(lambda tap: entry[tap, :, channels:])
        for j in range(2):
            block_w[d, j] = stacked(lambda tap: blocks[0, j, tap])

    for moment in range(ticks):
        padded[:, LANES:(TILES + 1) * LANES] = frames[moment]

        def keep(tile, sums):
            for d in range(2):
                pre[moment, d, :, at_tile(tile, 0)] = sums[d]

        convolve(padded, frame_w, keep)

    def advance(moment, d):
        receive(moment, d)
        warp(arrived[moment][d], (src_f, src_b)[d], moment, padded)

        def entered(tile, sums):
            value = lrelu(pre[moment, d, :, at_tile(tile, 0)] + sums[0])
            hidden[:, at_tile(tile, 1)] = value.astype(BF16)

        convolve(padded, warp_w.at[d], entered)

        def inside(tile, sums):
            inner[:, at_tile(tile, 1)] = lrelu(sums[0]).astype(BF16)

        convolve(hidden, block_w.at[d, 0], inside)

        def added(tile, sums):
            value = hidden[:, at_tile(tile, 1)].astype(F32) + sums[0]
            if moment < ticks - 1:
                state[d, :, at_tile(tile, 0)] = value.astype(BF16)
            else:
                (final_f, final_b)[d][:, at_tile(tile, 0)] = value.astype(BF16)

        convolve(inner, block_w.at[d, 1], added)

    def restore(moment):
        halves = (state.at[0], state.at[1]) if moment < ticks - 1 else (final_f, final_b)

        def step(group, _):
            lanes = pl.ds(pl.multiple_of(group * (GROUP * LANES), GROUP * LANES), GROUP * LANES)
            both = jnp.concatenate([halves[0][:, lanes], halves[1][:, lanes]], axis=0)
            mixed = jnp.dot(mixing[...], both, preferred_element_type=F32)
            restored[moment, :, lanes] = (frames[moment, :, lanes].astype(F32) + mixed).astype(BF16)
            return _

        lax.fori_loop(0, TILES // GROUP, step, 0)

    for moment in range(ticks):
        for d in range(2):
            advance(moment, d)
            if moment < ticks - 1:
                send(moment + 1, d)
        restore(moment)

    for moment in range(ticks):
        for d in range(2):
            for chunk in range(CHUNKS):
                @pl.when(has_to[d])
                def _():
                    sending(moment, d, chunk).wait_send()

                @pl.when(has_from[d])
                def _():
                    passing(moment, d, chunk).wait_send()


def shards(
    frames,
    forward_carry,
    backward_carry,
    forward_source,
    backward_source,
    forward_entry,
    forward_blocks,
    backward_entry,
    backward_blocks,
    mixing_weight,
):
    ticks, _, _, channels, pixels = frames.shape
    vmem = pl.BlockSpec(memory_space=pltpu.VMEM)
    smem = pl.BlockSpec(memory_space=pltpu.SMEM)
    flat = jax.ShapeDtypeStruct((channels, pixels), BF16)
    wide = pixels + 2 * LANES
    semaphores = pltpu.SemaphoreType.DMA((ticks, 2, CHUNKS))
    restored, final_f, final_b = pl.pallas_call(
        functools.partial(kernel, lax.axis_size("tm")),
        out_shape=(jax.ShapeDtypeStruct((ticks, channels, pixels), BF16), flat, flat),
        in_specs=[vmem] * 3 + [smem] * 2 + [vmem] * 5,
        out_specs=(vmem, vmem, vmem),
        scratch_shapes=[
            *[pltpu.VMEM((2, channels, pixels), BF16)] * (2 * ticks),
            pltpu.VMEM((2, channels, pixels), BF16),
            pltpu.VMEM((channels, wide), BF16),
            pltpu.VMEM((channels, wide), BF16),
            pltpu.VMEM((channels, wide), BF16),
            pltpu.VMEM((ticks, 2, channels, pixels), F32),
            pltpu.VMEM((6 * channels, 3 * channels), BF16),
            pltpu.VMEM((2, 3 * channels, 3 * channels), BF16),
            pltpu.VMEM((2, 2, 3 * channels, 3 * channels), BF16),
            semaphores,
            semaphores,
            semaphores,
            semaphores,
        ],
        compiler_params=pltpu.CompilerParams(collective_id=0, has_side_effects=True),
        name="propagate",
    )(
        frames.reshape(ticks, channels, pixels),
        forward_carry.reshape(channels, pixels),
        backward_carry.reshape(channels, pixels),
        forward_source.reshape(ticks, -1),
        backward_source.reshape(ticks, -1),
        forward_entry,
        forward_blocks,
        backward_entry,
        backward_blocks,
        mixing_weight,
    )
    return restored[:, None, None], final_f[None, None], final_b[None, None]


def solution(mesh):
    placed = (
        P(None, ("groups", "tm"), "tile", None, None),
        P(("groups", "tm"), "tile", None, None),
        P(("groups", "tm"), "tile", None, None),
        P(None, ("groups", "tm"), "tile"),
        P(None, ("groups", "tm"), "tile"),
        P(),
        P(),
        P(),
        P(),
        P(),
    )
    return jax.shard_map(
        shards,
        mesh=mesh,
        in_specs=placed,
        out_specs=(
            P(None, ("groups", "tm"), "tile", None, None),
            P(("groups", "tm"), "tile", None, None),
            P(("groups", "tm"), "tile", None, None),
        ),
        check_vma=False,
    )
```

```python
import functools

import jax
import jax.numpy as jnp
from jax import lax
from jax.experimental import pallas as pl
from jax.experimental.pallas import tpu as pltpu
from jax.sharding import PartitionSpec as P

RH = 32
RW = 64
BH = 8
BW = 16
LANES = 128
TILES = RH * RW // LANES
GROUP = 16
PACK = 16
CHUNKS = 2
MESH = pl.DeviceIdType.MESH
F32 = jnp.float32
BF16 = jnp.bfloat16


def lrelu(value):
    return jnp.maximum(value, 0.1 * value)


def stacked(piece):
    return jnp.concatenate(
        [jnp.concatenate([piece(3 * a + b) for a in range(3)], axis=1) for b in range(3)], axis=0
    )


def lane_of(rows):
    return lax.broadcasted_iota(jnp.int32, (rows, LANES), 1)


def convolve(source, weight, finish):
    channels = source.shape[0]
    lane = lane_of(channels)
    first_half = lane < RW
    column = lane % RW
    outs = weight.shape[0] // (3 * channels)

    def step(group, _):
        start = pl.multiple_of(group * (GROUP * LANES), GROUP * LANES)
        window = source[:, pl.ds(start, (GROUP + 2) * LANES)]
        tiles = [window[:, t * LANES:(t + 1) * LANES] for t in range(GROUP + 2)]
        turned = [pltpu.roll(tile, RW, 1) for tile in tiles]
        between = [jnp.where(first_half, turned[t], turned[t + 1]) for t in range(GROUP + 1)]
        rhs = jnp.concatenate(
            [
                jnp.concatenate(between[:-1], axis=1),
                jnp.concatenate(tiles[1:-1], axis=1),
                jnp.concatenate(between[1:], axis=1),
            ],
            axis=0,
        )
        product = jnp.dot(weight[...], rhs, preferred_element_type=F32)
        for t in range(GROUP):
            sums = []
            for o in range(outs):
                left, mid, right = (
                    product[(3 * o + b) * channels:(3 * o + b + 1) * channels, t * LANES:(t + 1) * LANES]
                    for b in range(3)
                )
                left = jnp.where(column == 0, 0.0, pltpu.roll(left, 1, 1))
                right = jnp.where(column == RW - 1, 0.0, pltpu.roll(right, LANES - 1, 1))
                sums.append(mid + left + right)
            finish(group * GROUP + t, sums)
        return _

    lax.fori_loop(0, TILES // GROUP, step, 0)


def at_tile(tile, padded):
    return pl.ds(pl.multiple_of((tile + padded) * LANES, LANES), LANES)


def turned_columns(tile, steps, lane):
    if steps == 0:
        return tile
    shift = steps * BW
    inside = pltpu.roll(tile, shift, 1)
    wrapped = pltpu.roll(tile, (shift - RW) % LANES, 1)
    return jnp.where(lane % RW >= shift, inside, wrapped)


def by_column(block_of_lane, values):
    spread = jnp.full(block_of_lane.shape, values[0], jnp.int32)
    for q in range(1, len(values)):
        spread = jnp.where(block_of_lane == q, values[q], spread)
    return spread


def warp(arrived, sources, moment, target):
    channels = target.shape[0]
    cols = RW // BW
    rows = RH // BH
    tiles_of_block = BH * RW // LANES
    lane = lane_of(PACK)
    block_of_lane = lane % RW // BW

    def step(row, _):
        regions, moves, turns = [], [], []
        for col in range(cols):
            block = sources[moment, row * cols + col]
            within = lax.rem(block, rows * cols)
            regions.append(lax.div(block, rows * cols))
            moves.append(lax.div(within, cols) - row)
            turns.append(lax.rem(col - lax.rem(within, cols) + cols, cols))
        turn = by_column(block_of_lane, turns)
        picks = []
        for steps in range(cols):
            order = [(q + steps) % cols for q in range(cols)]
            region = by_column(block_of_lane, [regions[c] for c in order])
            move = by_column(block_of_lane, [moves[c] for c in order])
            picks.append((region == 1, move < 0, move > 0, turn == steps))
        near = (jnp.maximum(row - 1, 0), row, jnp.minimum(row + 1, rows - 1))
        for t in range(tiles_of_block):
            for part in range(channels // PACK):
                held = pl.ds(part * PACK, PACK)
                tiles = [
                    [arrived[region, held, at_tile(near_row * tiles_of_block + t, 0)] for region in range(2)]
                    for near_row in near
                ]
                result = None
                for steps in range(cols):
                    second, above, below, wanted = picks[steps]
                    up, same, down = (jnp.where(second, pair[1], pair[0]) for pair in tiles)
                    moved = jnp.where(above, up, jnp.where(below, down, same))
                    moved = turned_columns(moved, steps, lane)
                    result = moved if result is None else jnp.where(wanted, moved, result)
                target[held, at_tile(row * tiles_of_block + t, 1)] = result
        return _

    lax.fori_loop(0, rows, step, 0)


def kernel(
    count,
    frames,
    carry_f,
    carry_b,
    src_f,
    src_b,
    entry_f,
    blocks_f,
    entry_b,
    blocks_b,
    mixing,
    restored,
    final_f,
    final_b,
    arrived_0f,
    arrived_0b,
    arrived_1f,
    arrived_1b,
    state,
    padded,
    hidden,
    inner,
    pre,
    frame_w,
    warp_w,
    block_w,
    send_sem,
    recv_sem,
    pass_sem,
    got_sem,
):
    ticks, channels, pixels = frames.shape
    arrived = ((arrived_0f, arrived_0b), (arrived_1f, arrived_1b))
    me = lax.axis_index("tm")
    side = lax.axis_index("tile")
    other = 1 - side
    to = (me + 1, me - 1)
    has_to = (me < count - 1, me > 0)
    has_from = (me > 0, me < count - 1)

    barrier = pltpu.get_barrier_semaphore()
    pl.semaphore_signal(barrier, inc=1, device_id={"tile": other}, device_id_type=MESH)
    for d in range(2):
        @pl.when(has_to[d])
        def _(d=d):
            pl.semaphore_signal(barrier, inc=1, device_id={"tm": to[d]}, device_id_type=MESH)
    pl.semaphore_wait(barrier, 1 + jnp.minimum(me, 1) + jnp.minimum(count - 1 - me, 1))

    part = channels // CHUNKS

    def sending(moment, d, chunk):
        rows = pl.ds(chunk * part, part)
        origin = (carry_f, carry_b)[d].at[rows] if moment == 0 else state.at[d, rows]
        return pltpu.make_async_remote_copy(
            src_ref=origin,
            dst_ref=arrived[moment][d].at[side, rows],
            send_sem=send_sem.at[moment, d, chunk],
            recv_sem=recv_sem.at[moment, d, chunk],
            device_id={"tm": to[d]},
            device_id_type=MESH,
        )

    def passing(moment, d, chunk):
        rows = pl.ds(chunk * part, part)
        return pltpu.make_async_remote_copy(
            src_ref=arrived[moment][d].at[side, rows],
            dst_ref=arrived[moment][d].at[side, rows],
            send_sem=pass_sem.at[moment, d, chunk],
            recv_sem=got_sem.at[moment, d, chunk],
            device_id={"tile": other},
            device_id_type=MESH,
        )

    def send(moment, d):
        @pl.when(has_to[d])
        def _():
            for chunk in range(CHUNKS):
                sending(moment, d, chunk).start()

    def receive(moment, d):
        @pl.when(has_from[d])
        def _():
            for chunk in range(CHUNKS):
                sending(moment, d, chunk).wait_recv()
                passing(moment, d, chunk).start()
            for chunk in range(CHUNKS):
                passing(moment, d, chunk).wait_recv()

    send(0, 0)
    send(0, 1)

    for d in range(2):
        @pl.when(jnp.logical_not(has_from[d]))
        def _(d=d):
            for moment in range(ticks):
                for region in range(2):
                    arrived[moment][d][region] = jnp.zeros((channels, pixels), BF16)
    edge = jnp.zeros((channels, LANES), BF16)
    for buffer in (padded, hidden, inner):
        buffer[:, :LANES] = edge
        buffer[:, (TILES + 1) * LANES:] = edge
    for d, (entry, blocks) in enumerate(((entry_f, blocks_f), (entry_b, blocks_b))):
        frame_w[3 * channels * d:3 * channels * (d + 1)] = stacked(lambda tap: entry[tap, :, :channels])
        warp_w[d] = stacked(lambda tap: entry[tap, :, channels:])
        for j in range(2):
            block_w[d, j] = stacked(lambda tap: blocks[0, j, tap])

    for moment in range(ticks):
        padded[:, LANES:(TILES + 1) * LANES] = frames[moment]

        def keep(tile, sums):
            for d in range(2):
                pre[moment, d, :, at_tile(tile, 0)] = sums[d]

        convolve(padded, frame_w, keep)

    def advance(moment, d):
        receive(moment, d)
        warp(arrived[moment][d], (src_f, src_b)[d], moment, padded)

        def entered(tile, sums):
            value = lrelu(pre[moment, d, :, at_tile(tile, 0)] + sums[0])
            hidden[:, at_tile(tile, 1)] = value.astype(BF16)

        convolve(padded, warp_w.at[d], entered)

        def inside(tile, sums):
            inner[:, at_tile(tile, 1)] = lrelu(sums[0]).astype(BF16)

        convolve(hidden, block_w.at[d, 0], inside)

        def added(tile, sums):
            value = hidden[:, at_tile(tile, 1)].astype(F32) + sums[0]
            if moment < ticks - 1:
                state[d, :, at_tile(tile, 0)] = value.astype(BF16)
            else:
                (final_f, final_b)[d][:, at_tile(tile, 0)] = value.astype(BF16)

        convolve(inner, block_w.at[d, 1], added)

    def restore(moment):
        halves = (state.at[0], state.at[1]) if moment < ticks - 1 else (final_f, final_b)

        def step(group, _):
            lanes = pl.ds(pl.multiple_of(group * (GROUP * LANES), GROUP * LANES), GROUP * LANES)
            both = jnp.concatenate([halves[0][:, lanes], halves[1][:, lanes]], axis=0)
            mixed = jnp.dot(mixing[...], both, preferred_element_type=F32)
            restored[moment, :, lanes] = (frames[moment, :, lanes].astype(F32) + mixed).astype(BF16)
            return _

        lax.fori_loop(0, TILES // GROUP, step, 0)

    for moment in range(ticks):
        for d in range(2):
            advance(moment, d)
            if moment < ticks - 1:
                send(moment + 1, d)
        restore(moment)

    for moment in range(ticks):
        for d in range(2):
            for chunk in range(CHUNKS):
                @pl.when(has_to[d])
                def _():
                    sending(moment, d, chunk).wait_send()

                @pl.when(has_from[d])
                def _():
                    passing(moment, d, chunk).wait_send()


def hand_over(*refs):
    third = len(refs) // 4
    given, out, held = refs[:third], refs[third:2 * third], refs[2 * third:3 * third]
    sems = refs[3 * third:]
    taken = [pltpu.make_async_copy(g, h, s.at[0]) for g, h, s in zip(given, held, sems)]
    put = [pltpu.make_async_copy(h, o, s.at[1]) for h, o, s in zip(held, out, sems)]
    for copy in taken:
        copy.start()
    for first, second in zip(taken, put):
        first.wait()
        second.start()
    for copy in put:
        copy.wait()


def shards(
    frames,
    forward_carry,
    backward_carry,
    forward_source,
    backward_source,
    forward_entry,
    forward_blocks,
    backward_entry,
    backward_blocks,
    mixing_weight,
):
    ticks, _, _, channels, pixels = frames.shape
    vmem = pl.BlockSpec(memory_space=pltpu.VMEM)
    smem = pl.BlockSpec(memory_space=pltpu.SMEM)
    flat = jax.ShapeDtypeStruct((channels, pixels), BF16)
    wide = pixels + 2 * LANES
    semaphores = pltpu.SemaphoreType.DMA((ticks, 2, CHUNKS))
    restored, final_f, final_b = pl.pallas_call(
        functools.partial(kernel, lax.axis_size("tm")),
        out_shape=(jax.ShapeDtypeStruct((ticks, channels, pixels), BF16), flat, flat),
        in_specs=[vmem] * 3 + [smem] * 2 + [vmem] * 5,
        out_specs=(vmem, vmem, vmem),
        scratch_shapes=[
            *[pltpu.VMEM((2, channels, pixels), BF16)] * (2 * ticks),
            pltpu.VMEM((2, channels, pixels), BF16),
            pltpu.VMEM((channels, wide), BF16),
            pltpu.VMEM((channels, wide), BF16),
            pltpu.VMEM((channels, wide), BF16),
            pltpu.VMEM((ticks, 2, channels, pixels), F32),
            pltpu.VMEM((6 * channels, 3 * channels), BF16),
            pltpu.VMEM((2, 3 * channels, 3 * channels), BF16),
            pltpu.VMEM((2, 2, 3 * channels, 3 * channels), BF16),
            semaphores,
            semaphores,
            semaphores,
            semaphores,
        ],
        compiler_params=pltpu.CompilerParams(collective_id=0, has_side_effects=True),
        name="propagate",
    )(
        frames.reshape(ticks, channels, pixels),
        forward_carry.reshape(channels, pixels),
        backward_carry.reshape(channels, pixels),
        forward_source.reshape(ticks, -1),
        backward_source.reshape(ticks, -1),
        forward_entry,
        forward_blocks,
        backward_entry,
        backward_blocks,
        mixing_weight,
    )
    results = (restored, final_f, final_b)
    anywhere = pl.BlockSpec(memory_space=pl.ANY)
    restored, final_f, final_b = pl.pallas_call(
        hand_over,
        out_shape=tuple(jax.ShapeDtypeStruct(r.shape, r.dtype) for r in results),
        in_specs=[anywhere] * len(results),
        out_specs=(anywhere,) * len(results),
        scratch_shapes=[pltpu.VMEM(r.shape, r.dtype) for r in results]
        + [pltpu.SemaphoreType.DMA((2,))] * len(results),
        name="hand_over",
    )(*results)
    return restored[:, None, None], final_f[None, None], final_b[None, None]


def solution(mesh):
    placed = (
        P(None, ("groups", "tm"), "tile", None, None),
        P(("groups", "tm"), "tile", None, None),
        P(("groups", "tm"), "tile", None, None),
        P(None, ("groups", "tm"), "tile"),
        P(None, ("groups", "tm"), "tile"),
        P(),
        P(),
        P(),
        P(),
        P(),
    )
    return jax.shard_map(
        shards,
        mesh=mesh,
        in_specs=placed,
        out_specs=(
            P(None, ("groups", "tm"), "tile", None, None),
            P(("groups", "tm"), "tile", None, None),
            P(("groups", "tm"), "tile", None, None),
        ),
        check_vma=False,
    )
```

```python
import functools

import jax
import jax.numpy as jnp
from jax import lax
from jax.experimental import pallas as pl
from jax.experimental.pallas import tpu as pltpu
from jax.sharding import PartitionSpec as P

RH = 32
RW = 64
BH = 8
BW = 16
LANES = 128
TILES = RH * RW // LANES
GROUP = 16
PACK = 16
CHUNKS = 2
MESH = pl.DeviceIdType.MESH
F32 = jnp.float32
BF16 = jnp.bfloat16


def lrelu(value):
    return jnp.maximum(value, 0.1 * value)


def stacked(piece):
    return jnp.concatenate(
        [jnp.concatenate([piece(3 * a + b) for a in range(3)], axis=1) for b in range(3)], axis=0
    )


def lane_of(rows):
    return lax.broadcasted_iota(jnp.int32, (rows, LANES), 1)


def convolve(source, weight, finish):
    channels = source.shape[0]
    lane = lane_of(channels)
    first_half = lane < RW
    column = lane % RW
    outs = weight.shape[0] // (3 * channels)

    def step(group, _):
        start = pl.multiple_of(group * (GROUP * LANES), GROUP * LANES)
        window = source[:, pl.ds(start, (GROUP + 2) * LANES)]
        tiles = [window[:, t * LANES:(t + 1) * LANES] for t in range(GROUP + 2)]
        turned = [pltpu.roll(tile, RW, 1) for tile in tiles]
        between = [jnp.where(first_half, turned[t], turned[t + 1]) for t in range(GROUP + 1)]
        rhs = jnp.concatenate(
            [
                jnp.concatenate(between[:-1], axis=1),
                jnp.concatenate(tiles[1:-1], axis=1),
                jnp.concatenate(between[1:], axis=1),
            ],
            axis=0,
        )
        product = jnp.dot(weight[...], rhs, preferred_element_type=F32)
        for t in range(GROUP):
            sums = []
            for o in range(outs):
                left, mid, right = (
                    product[(3 * o + b) * channels:(3 * o + b + 1) * channels, t * LANES:(t + 1) * LANES]
                    for b in range(3)
                )
                left = jnp.where(column == 0, 0.0, pltpu.roll(left, 1, 1))
                right = jnp.where(column == RW - 1, 0.0, pltpu.roll(right, LANES - 1, 1))
                sums.append(mid + left + right)
            finish(group * GROUP + t, sums)
        return _

    lax.fori_loop(0, TILES // GROUP, step, 0)


def at_tile(tile, padded):
    return pl.ds(pl.multiple_of((tile + padded) * LANES, LANES), LANES)


def turned_columns(tile, steps, lane):
    if steps == 0:
        return tile
    shift = steps * BW
    inside = pltpu.roll(tile, shift, 1)
    wrapped = pltpu.roll(tile, (shift - RW) % LANES, 1)
    return jnp.where(lane % RW >= shift, inside, wrapped)


def by_column(block_of_lane, values):
    spread = jnp.full(block_of_lane.shape, values[0], jnp.int32)
    for q in range(1, len(values)):
        spread = jnp.where(block_of_lane == q, values[q], spread)
    return spread


def warp(arrived, sources, moment, target):
    channels = target.shape[0]
    cols = RW // BW
    rows = RH // BH
    tiles_of_block = BH * RW // LANES
    lane = lane_of(PACK)
    block_of_lane = lane % RW // BW

    def step(row, _):
        regions, moves, turns = [], [], []
        for col in range(cols):
            block = sources[moment, row * cols + col]
            within = lax.rem(block, rows * cols)
            regions.append(lax.div(block, rows * cols))
            moves.append(lax.div(within, cols) - row)
            turns.append(lax.rem(col - lax.rem(within, cols) + cols, cols))
        turn = by_column(block_of_lane, turns)
        picks = []
        for steps in range(cols):
            order = [(q + steps) % cols for q in range(cols)]
            region = by_column(block_of_lane, [regions[c] for c in order])
            move = by_column(block_of_lane, [moves[c] for c in order])
            picks.append((region == 1, move < 0, move > 0, turn == steps))
        near = (jnp.maximum(row - 1, 0), row, jnp.minimum(row + 1, rows - 1))
        for t in range(tiles_of_block):
            for part in range(channels // PACK):
                held = pl.ds(part * PACK, PACK)
                tiles = [
                    [arrived[region, held, at_tile(near_row * tiles_of_block + t, 0)] for region in range(2)]
                    for near_row in near
                ]
                result = None
                for steps in range(cols):
                    second, above, below, wanted = picks[steps]
                    up, same, down = (jnp.where(second, pair[1], pair[0]) for pair in tiles)
                    moved = jnp.where(above, up, jnp.where(below, down, same))
                    moved = turned_columns(moved, steps, lane)
                    result = moved if result is None else jnp.where(wanted, moved, result)
                target[held, at_tile(row * tiles_of_block + t, 1)] = result
        return _

    lax.fori_loop(0, rows, step, 0, unroll=True)


def kernel(
    count,
    frames,
    carry_f,
    carry_b,
    src_f,
    src_b,
    entry_f,
    blocks_f,
    entry_b,
    blocks_b,
    mixing,
    restored,
    final_f,
    final_b,
    arrived_0f,
    arrived_0b,
    arrived_1f,
    arrived_1b,
    state,
    padded,
    hidden,
    inner,
    pre,
    frame_w,
    warp_w,
    block_w,
    send_sem,
    recv_sem,
    pass_sem,
    got_sem,
):
    ticks, channels, pixels = frames.shape
    arrived = ((arrived_0f, arrived_0b), (arrived_1f, arrived_1b))
    me = lax.axis_index("tm")
    side = lax.axis_index("tile")
    other = 1 - side
    to = (me + 1, me - 1)
    has_to = (me < count - 1, me > 0)
    has_from = (me > 0, me < count - 1)

    barrier = pltpu.get_barrier_semaphore()
    pl.semaphore_signal(barrier, inc=1, device_id={"tile": other}, device_id_type=MESH)
    for d in range(2):
        @pl.when(has_to[d])
        def _(d=d):
            pl.semaphore_signal(barrier, inc=1, device_id={"tm": to[d]}, device_id_type=MESH)
    pl.semaphore_wait(barrier, 1 + jnp.minimum(me, 1) + jnp.minimum(count - 1 - me, 1))

    part = channels // CHUNKS

    def sending(moment, d, chunk):
        rows = pl.ds(chunk * part, part)
        origin = (carry_f, carry_b)[d].at[rows] if moment == 0 else state.at[d, rows]
        return pltpu.make_async_remote_copy(
            src_ref=origin,
            dst_ref=arrived[moment][d].at[side, rows],
            send_sem=send_sem.at[moment, d, chunk],
            recv_sem=recv_sem.at[moment, d, chunk],
            device_id={"tm": to[d]},
            device_id_type=MESH,
        )

    def passing(moment, d, chunk):
        rows = pl.ds(chunk * part, part)
        return pltpu.make_async_remote_copy(
            src_ref=arrived[moment][d].at[side, rows],
            dst_ref=arrived[moment][d].at[side, rows],
            send_sem=pass_sem.at[moment, d, chunk],
            recv_sem=got_sem.at[moment, d, chunk],
            device_id={"tile": other},
            device_id_type=MESH,
        )

    def send(moment, d):
        @pl.when(has_to[d])
        def _():
            for chunk in range(CHUNKS):
                sending(moment, d, chunk).start()

    def receive(moment, d):
        @pl.when(has_from[d])
        def _():
            for chunk in range(CHUNKS):
                sending(moment, d, chunk).wait_recv()
                passing(moment, d, chunk).start()
            for chunk in range(CHUNKS):
                passing(moment, d, chunk).wait_recv()

    send(0, 0)
    send(0, 1)

    for d in range(2):
        @pl.when(jnp.logical_not(has_from[d]))
        def _(d=d):
            for moment in range(ticks):
                for region in range(2):
                    arrived[moment][d][region] = jnp.zeros((channels, pixels), BF16)
    edge = jnp.zeros((channels, LANES), BF16)
    for buffer in (padded, hidden, inner):
        buffer[:, :LANES] = edge
        buffer[:, (TILES + 1) * LANES:] = edge
    for d, (entry, blocks) in enumerate(((entry_f, blocks_f), (entry_b, blocks_b))):
        frame_w[3 * channels * d:3 * channels * (d + 1)] = stacked(lambda tap: entry[tap, :, :channels])
        warp_w[d] = stacked(lambda tap: entry[tap, :, channels:])
        for j in range(2):
            block_w[d, j] = stacked(lambda tap: blocks[0, j, tap])

    for moment in range(ticks):
        padded[:, LANES:(TILES + 1) * LANES] = frames[moment]

        def keep(tile, sums):
            for d in range(2):
                pre[moment, d, :, at_tile(tile, 0)] = sums[d]

        convolve(padded, frame_w, keep)

    def advance(moment, d):
        receive(moment, d)
        warp(arrived[moment][d], (src_f, src_b)[d], moment, padded)

        def entered(tile, sums):
            value = lrelu(pre[moment, d, :, at_tile(tile, 0)] + sums[0])
            hidden[:, at_tile(tile, 1)] = value.astype(BF16)

        convolve(padded, warp_w.at[d], entered)

        def inside(tile, sums):
            inner[:, at_tile(tile, 1)] = lrelu(sums[0]).astype(BF16)

        convolve(hidden, block_w.at[d, 0], inside)

        def added(tile, sums):
            value = hidden[:, at_tile(tile, 1)].astype(F32) + sums[0]
            if moment < ticks - 1:
                state[d, :, at_tile(tile, 0)] = value.astype(BF16)
            else:
                (final_f, final_b)[d][:, at_tile(tile, 0)] = value.astype(BF16)

        convolve(inner, block_w.at[d, 1], added)

    def restore(moment):
        halves = (state.at[0], state.at[1]) if moment < ticks - 1 else (final_f, final_b)

        def step(group, _):
            lanes = pl.ds(pl.multiple_of(group * (GROUP * LANES), GROUP * LANES), GROUP * LANES)
            both = jnp.concatenate([halves[0][:, lanes], halves[1][:, lanes]], axis=0)
            mixed = jnp.dot(mixing[...], both, preferred_element_type=F32)
            restored[moment, :, lanes] = (frames[moment, :, lanes].astype(F32) + mixed).astype(BF16)
            return _

        lax.fori_loop(0, TILES // GROUP, step, 0)

    for moment in range(ticks):
        for d in range(2):
            advance(moment, d)
            if moment < ticks - 1:
                send(moment + 1, d)
        restore(moment)

    for moment in range(ticks):
        for d in range(2):
            for chunk in range(CHUNKS):
                @pl.when(has_to[d])
                def _():
                    sending(moment, d, chunk).wait_send()

                @pl.when(has_from[d])
                def _():
                    passing(moment, d, chunk).wait_send()


def hand_over(*refs):
    third = len(refs) // 4
    given, out, held = refs[:third], refs[third:2 * third], refs[2 * third:3 * third]
    sems = refs[3 * third:]
    taken = [pltpu.make_async_copy(g, h, s.at[0]) for g, h, s in zip(given, held, sems)]
    put = [pltpu.make_async_copy(h, o, s.at[1]) for h, o, s in zip(held, out, sems)]
    for copy in taken:
        copy.start()
    for first, second in zip(taken, put):
        first.wait()
        second.start()
    for copy in put:
        copy.wait()


def shards(
    frames,
    forward_carry,
    backward_carry,
    forward_source,
    backward_source,
    forward_entry,
    forward_blocks,
    backward_entry,
    backward_blocks,
    mixing_weight,
):
    ticks, _, _, channels, pixels = frames.shape
    vmem = pl.BlockSpec(memory_space=pltpu.VMEM)
    smem = pl.BlockSpec(memory_space=pltpu.SMEM)
    flat = jax.ShapeDtypeStruct((channels, pixels), BF16)
    wide = pixels + 2 * LANES
    semaphores = pltpu.SemaphoreType.DMA((ticks, 2, CHUNKS))
    restored, final_f, final_b = pl.pallas_call(
        functools.partial(kernel, lax.axis_size("tm")),
        out_shape=(jax.ShapeDtypeStruct((ticks, channels, pixels), BF16), flat, flat),
        in_specs=[vmem] * 3 + [smem] * 2 + [vmem] * 5,
        out_specs=(vmem, vmem, vmem),
        scratch_shapes=[
            *[pltpu.VMEM((2, channels, pixels), BF16)] * (2 * ticks),
            pltpu.VMEM((2, channels, pixels), BF16),
            pltpu.VMEM((channels, wide), BF16),
            pltpu.VMEM((channels, wide), BF16),
            pltpu.VMEM((channels, wide), BF16),
            pltpu.VMEM((ticks, 2, channels, pixels), F32),
            pltpu.VMEM((6 * channels, 3 * channels), BF16),
            pltpu.VMEM((2, 3 * channels, 3 * channels), BF16),
            pltpu.VMEM((2, 2, 3 * channels, 3 * channels), BF16),
            semaphores,
            semaphores,
            semaphores,
            semaphores,
        ],
        compiler_params=pltpu.CompilerParams(collective_id=0, has_side_effects=True),
        name="propagate",
    )(
        frames.reshape(ticks, channels, pixels),
        forward_carry.reshape(channels, pixels),
        backward_carry.reshape(channels, pixels),
        forward_source.reshape(ticks, -1),
        backward_source.reshape(ticks, -1),
        forward_entry,
        forward_blocks,
        backward_entry,
        backward_blocks,
        mixing_weight,
    )
    results = (restored, final_f, final_b)
    anywhere = pl.BlockSpec(memory_space=pl.ANY)
    restored, final_f, final_b = pl.pallas_call(
        hand_over,
        out_shape=tuple(jax.ShapeDtypeStruct(r.shape, r.dtype) for r in results),
        in_specs=[anywhere] * len(results),
        out_specs=(anywhere,) * len(results),
        scratch_shapes=[pltpu.VMEM(r.shape, r.dtype) for r in results]
        + [pltpu.SemaphoreType.DMA((2,))] * len(results),
        name="hand_over",
    )(*results)
    return restored[:, None, None], final_f[None, None], final_b[None, None]


def solution(mesh):
    placed = (
        P(None, ("groups", "tm"), "tile", None, None),
        P(("groups", "tm"), "tile", None, None),
        P(("groups", "tm"), "tile", None, None),
        P(None, ("groups", "tm"), "tile"),
        P(None, ("groups", "tm"), "tile"),
        P(),
        P(),
        P(),
        P(),
        P(),
    )
    return jax.shard_map(
        shards,
        mesh=mesh,
        in_specs=placed,
        out_specs=(
            P(None, ("groups", "tm"), "tile", None, None),
            P(("groups", "tm"), "tile", None, None),
            P(("groups", "tm"), "tile", None, None),
        ),
        check_vma=False,
    )
```
